128 devices in a mesh: row: 8 (over z, core), col: 16 (over x, y).
Axes of the slice: x: 4, y: 4, z: 4, core: 2. Of those that a mesh axis runs over, the one named last changes fastest.
Arguments:
- valence: bfloat16 [128, 2, 64000], P(('row', 'col')), may hold values from -2.09375 to 2.09375
- conduction: bfloat16 [512, 2, 64000], P(('row', 'col')), may hold values from -2.09375 to 2.09375
- valence_slot_index: int32 [2], replicated, may hold values from 0 to 127
- weights: float32 [2, 512], P(None, ('row', 'col')), may hold values from 0.1 to 1
- sphere_index: int32 [9984], replicated, may hold values from 0 to 63999, as said below
Outputs:
- polarizability: float32 [2, 9984, 9984], P(None, 'row', 'col')
The draws below stay inside these ranges and needn't reach their ends.
Inputs may be any that keep to these rules, and one draw needn't show every extreme that they name: `sphere_index`: all entries are distinct.
All inputs are finite; a program needn't handle non-finite values.
Results may differ from the reference program's by a relative error of at most 0.0039.
Values may be sent and summed in bfloat16 or wider, within the bound.
No kernel may reach another device: no remote copies, remote signals or barrier semaphores. Data moves between devices by JAX's collectives and lax.ppermute only.
A program may use at most 256 MiB of HBM per device.

```python
import math
import jax
import jax.numpy as jnp

NBOX = 40
NG = 9984
WINDOW_VALENCE = 2
GRID_POINTS = 64000
NC = 512
VALENCE_SLOTS = 128


def draw_sphere_index(key, part):
    first = jax.random.fold_in(key, 11)
    second = jax.random.fold_in(key, 23)
    inner = 1 + jax.random.permutation(first, NBOX ** 3 - 2)[:NG - 2]
    ends = jnp.array([0, NBOX ** 3 - 1], dtype=jnp.int32)
    joined = jnp.concatenate([ends, inner.astype(jnp.int32)])
    return jax.random.permutation(second, joined).astype(jnp.int32)


def shard_levels(stream_key, shape, pieces, low, high):
    factor_of, own = 1.0, jax.random.fold_in(stream_key, 6)
    for position, shards_of in pieces:
        heights = jnp.exp(jax.random.uniform(jax.random.fold_in(own, position), (shards_of,), jnp.float32, low / len(pieces), high / len(pieces)))
        factor_of = factor_of * jnp.repeat(heights, shape[position] // shards_of).reshape([-1 if axis == position else 1 for axis in range(len(shape))])
    return factor_of


def noise(key, dims, width, most, shards=(), kind=jnp.bfloat16):
    result = jax.random.normal(key, dims, jnp.float32) * width
    if len(shards) > 0:
        result = shard_levels(key, dims, shards, -0.22, 0.18) * result
    return jnp.clip(result, min=-most, max=most).astype(kind)


def setup_inputs(seed: int = 0) -> dict:
    arg_keys = jax.random.split(jax.random.key(seed), 6)
    valence = noise(arg_keys[0], (VALENCE_SLOTS, 2, GRID_POINTS), 0.35, 2.09375, ((0, 128),))
    conduction = noise(arg_keys[1], (NC, 2, GRID_POINTS), 0.35, 2.09375, ((0, 128),))
    valence_slot_index = jax.random.randint(arg_keys[2], (WINDOW_VALENCE,), 0, VALENCE_SLOTS).astype(jnp.int32)
    weights = jnp.clip(jnp.exp(math.log(1.0) - 2.3025851 * jax.random.uniform(arg_keys[3], (WINDOW_VALENCE, NC), jnp.float32) ** shard_levels(arg_keys[3], (WINDOW_VALENCE, NC), ((1, 128),), -0.2, 0.2)), 0.1, 1.0)
    sphere_index = draw_sphere_index(jax.random.fold_in(arg_keys[5], 71), 0)
    return dict(valence=valence, conduction=conduction, valence_slot_index=valence_slot_index, weights=weights, sphere_index=sphere_index)


def reference(valence, conduction, valence_slot_index, weights, sphere_index):
    chosen = valence[valence_slot_index].astype(jnp.float32)
    states = conduction.astype(jnp.float32)
    val_re = chosen[:, 0][:, None, :]
    val_im = chosen[:, 1][:, None, :]
    con_re = states[:, 0][None, :, :]
    con_im = states[:, 1][None, :, :]
    dens_re = val_re * con_re + val_im * con_im
    dens_im = val_re * con_im - val_im * con_re
    field = (dens_re + 1j * dens_im).reshape(WINDOW_VALENCE, NC, NBOX, NBOX, NBOX)
    spectrum = jnp.fft.fftn(field, axes=(2, 3, 4), norm="ortho").reshape(WINDOW_VALENCE, NC, GRID_POINTS)
    picked = spectrum[:, :, sphere_index]
    values = jnp.stack([jnp.real(picked), jnp.imag(picked)], axis=2).astype(jnp.float32)
    plain = values.astype(jnp.bfloat16).reshape(WINDOW_VALENCE * NC, 2, NG)
    scaled = (weights[:, :, None, None] * values).astype(jnp.bfloat16).reshape(WINDOW_VALENCE * NC, 2, NG)
    left = jnp.transpose(scaled, (1, 0, 2)).reshape(2 * WINDOW_VALENCE * NC, NG)
    right = jnp.transpose(plain, (1, 0, 2)).reshape(2 * WINDOW_VALENCE * NC, NG)
    real_part = jnp.dot(left.T, right, preferred_element_type=jnp.float32)
    imag_part = jnp.dot(scaled[:, 1].T, plain[:, 0], preferred_element_type=jnp.float32) - jnp.dot(scaled[:, 0].T, plain[:, 1], preferred_element_type=jnp.float32)
    return jnp.stack([real_part, imag_part])
```

```python
import math
import numpy as np
import jax
import jax.numpy as jnp
from jax import lax
from jax.experimental import pallas as pl
from jax.experimental.pallas import tpu as pltpu
from jax.sharding import PartitionSpec as P

N = 40
LW = 384
LT = LW // 128
NB = 16
GB = 624
GP = 640

def split(x):
    hi = x.astype(jnp.bfloat16)
    lo = (x - hi.astype(jnp.float32)).astype(jnp.bfloat16)
    return hi, lo

def np_split(x):
    x = np.asarray(x, np.float32)
    hi = x.astype(jnp.bfloat16)
    lo = (x - hi.astype(np.float32)).astype(jnp.bfloat16)
    return hi, lo

def tables(nv, nc):
    k = np.arange(N)
    ang = 2 * np.pi * ((k[:, None] * k[None, :]) % N) / N
    c, s = np.cos(ang) / math.sqrt(N), np.sin(ang) / math.sqrt(N)
    f = np.block([[c, s], [-s, c]])
    hi, lo = np_split(f)
    axis = np.concatenate([hi, hi, lo], axis=1)
    pairs = nv * nc
    m = np.zeros((2, LW, N * 2 * pairs))
    for p in range(pairs):
        for comp in range(2):
            cols = np.arange(N) * 2 * pairs + comp * pairs + p
            for part in range(2):
                blk = f[comp * N:(comp + 1) * N, part * N:(part + 1) * N]
                m[part, p * N:(p + 1) * N][:, cols] = blk.T
    m = m.reshape(2 * LW, -1)
    mhi, mlo = np_split(m)
    last = np.stack([mhi, mlo])
    ident = np.eye(N)
    rp = np.zeros((nv * N, LW)); rq = np.zeros((nc * N, LW))
    for v in range(nv):
        for b in range(nc):
            p = v * nc + b
            rp[v * N:(v + 1) * N, p * N:(p + 1) * N] = ident
            rq[b * N:(b + 1) * N, p * N:(p + 1) * N] = ident
    return axis, last, rp.astype(jnp.bfloat16), rq.astype(jnp.bfloat16)

def stack3(x):
    hi, lo = split(x)
    return jnp.concatenate([hi, lo, hi], axis=0)

def pick_kernel(addr, p_ref, q_ref, sel_ref, w_ref, axis_ref, last_ref, rp_ref, plain_ref, scaled_ref, d_ref, z_ref, s_ref, t_ref):
    f32 = jnp.float32
    sq = N * N
    tdims = (((0,), (0,)), ((), ()))
    pre = lax.dot_general(p_ref[0], rp_ref[...], tdims, preferred_element_type=f32)[:sq]
    pim = lax.dot_general(p_ref[1], rp_ref[...], tdims, preferred_element_type=f32)[:sq]
    qre, qim = q_ref[0].astype(f32), q_ref[1].astype(f32)
    d_ref[0] = pre * qre + pim * qim
    d_ref[1] = pre * qim - pim * qre

    def over_e(b, _):
        rows = pl.ds(pl.multiple_of(b * N, 8), N)
        x = jnp.concatenate([d_ref[0, rows, :], d_ref[1, rows, :]], axis=0)
        y = jnp.dot(axis_ref[...], stack3(x), preferred_element_type=f32)
        for c in range(2):
            for l in range(LT):
                z_ref[c, l, rows, :] = y[c * N:(c + 1) * N, l * 128:(l + 1) * 128]
        return 0
    lax.fori_loop(0, N, over_e, 0, unroll=4)

    def over_b(k, _):
        rows = pl.ds(pl.multiple_of(k * N, 8), N)
        parts = []
        for c in range(2):
            parts.append(jnp.concatenate([z_ref[c, l, pl.ds(k, N, stride=N), :] for l in range(LT)], axis=1))
        x = jnp.concatenate(parts, axis=0)
        y = jnp.dot(axis_ref[...], stack3(x), preferred_element_type=f32)
        d_ref[0, rows, :] = y[:N]
        d_ref[1, rows, :] = y[N:]
        return 0
    lax.fori_loop(0, N, over_b, 0, unroll=4)

    chunk = 320
    def over_a(i, _):
        start = pl.multiple_of(i * chunk, 8)
        x = jnp.concatenate([d_ref[0, pl.ds(start, chunk), :], d_ref[1, pl.ds(start, chunk), :]], axis=1)
        hi, lo = split(x)
        y = jnp.dot(hi, last_ref[0], preferred_element_type=f32)
        y += jnp.dot(lo, last_ref[0], preferred_element_type=f32)
        y += jnp.dot(hi, last_ref[1], preferred_element_type=f32)
        for n in range(5):
            s_ref[pl.ds(pl.multiple_of(start + n * sq, 8), chunk), :] = y[:, n * 128:(n + 1) * 128]
        return 0
    lax.fori_loop(0, sq // chunk, over_a, 0)

    for j in range(NB):
        def pick(i, _, j=j):
            base = i * 16
            for u in range(16):
                t_ref[pl.ds(base + u, 1), :] = s_ref[pl.ds(addr[j * GB + base + u], 1), :]
            return 0
        lax.fori_loop(0, GB // 16, pick, 0)
        tt = t_ref[...].T
        sel = sel_ref[j]
        acc = jnp.zeros((16, GP), f32)
        for grp in range(8):
            acc = jnp.where(sel == grp, tt[16 * grp:16 * grp + 16], acc)
        plain_ref[j] = acc.astype(jnp.bfloat16)
        scaled_ref[j] = (acc * w_ref[...]).astype(jnp.bfloat16)

def pick_call(p, q, weights, sphere_index, tabs):
    axis, last, rp, _ = tabs
    sq = N * N
    ka, rest = sphere_index // sq, sphere_index % sq
    kb, ke = rest // N, rest % N
    addr = (ka // 8) * sq + ke * N + kb
    sel = jnp.pad((ka % 8).reshape(NB, 1, GB), ((0, 0), (0, 0), (0, GP - GB)), constant_values=-1)
    w = jnp.concatenate([weights, weights]).reshape(16, 1)
    vm = pl.BlockSpec(memory_space=pltpu.VMEM)
    out = jax.ShapeDtypeStruct((NB, 16, GP), jnp.bfloat16)
    return pl.pallas_call(
        pick_kernel,
        out_shape=(out, out),
        in_specs=[pl.BlockSpec(memory_space=pltpu.SMEM)] + [vm] * 7,
        out_specs=(vm, vm),
        scratch_shapes=[
            pltpu.VMEM((2, sq, LW), jnp.float32),
            pltpu.VMEM((2, LT, sq, 128), jnp.float32),
            pltpu.VMEM((5 * sq, 128), jnp.float32),
            pltpu.VMEM((GP, 128), jnp.float32),
        ],
        name="pick",
    )(addr, p, q, sel, w, jnp.asarray(axis), jnp.asarray(last), jnp.asarray(rp))

def expand_q(conduction, nv):
    nc = conduction.shape[0]
    sq = N * N
    q = conduction.reshape(nc, 2, N, sq).transpose(1, 3, 0, 2).reshape(2, sq, nc * N)
    q = jnp.concatenate([q] * nv, axis=2)
    return jnp.pad(q, ((0, 0), (0, 0), (0, LW - q.shape[2])))

def arrange_p(bands):
    nv = bands.shape[0]
    p = bands.reshape(nv, 2, N, N * N).transpose(1, 0, 2, 3).reshape(2, nv * N, N * N)
    return jnp.pad(p, ((0, 0), (0, 0), (0, 64)))

BOTH = ("row", "col")

def fetch_bands(stored, valence_slot_index):
    devices = lax.axis_size("row") * lax.axis_size("col")
    pieces = jnp.pad(stored.reshape(-1, 128), ((0, 24), (0, 0))).reshape(devices, 8, 128)
    pieces = lax.all_to_all(pieces, BOTH, 0, 0, tiled=True)
    mine = jnp.stack([lax.dynamic_index_in_dim(pieces, valence_slot_index[v], 0, keepdims=False) for v in range(2)])
    copies = jnp.broadcast_to(mine, (devices, *mine.shape))
    spread = lax.all_to_all(copies, BOTH, 0, 0, tiled=True)
    flat = spread.transpose(1, 0, 2, 3).reshape(2, -1, 128)[:, :1000]
    return flat.reshape(2, 2, N ** 3)

def product_kernel(left_ref, right_ref, out_ref):
    f32 = jnp.float32
    tdims = (((0,), (0,)), ((), ()))
    depth = left_ref.shape[0] * left_ref.shape[1] * 16
    right = right_ref[...]
    wide = right.astype(f32)
    turned = jnp.concatenate([-wide[:, :, 8:], wide[:, :, :8]], axis=2).astype(jnp.bfloat16)
    right = jnp.swapaxes(right, 0, 1).reshape(depth, GP)
    turned = jnp.swapaxes(turned, 0, 1).reshape(depth, GP)

    @pl.when(pl.program_id(0) == 0)
    def _():
        out_ref[...] = jnp.zeros_like(out_ref)

    for j in range(2):
        left = left_ref[:, :, j].reshape(depth, GP)
        for part, other in ((0, right), (1, turned)):
            y = lax.dot_general(left, other, tdims, preferred_element_type=f32)
            out_ref[part, j * GB:(j + 1) * GB, :] += y[:GB, :GB]

def product(left, right):
    cols, rows = left.shape[:2]
    step = 4
    return pl.pallas_call(
        product_kernel,
        out_shape=jax.ShapeDtypeStruct((2, 2 * GB, GB), jnp.float32),
        grid=(cols // step,),
        in_specs=[
            pl.BlockSpec((step, rows, 2, 16, GP), lambda i: (i, 0, 0, 0, 0)),
            pl.BlockSpec((rows, step, 16, GP), lambda i: (0, i, 0, 0)),
        ],
        out_specs=pl.BlockSpec((2, 2 * GB, GB), lambda i: (0, 0, 0)),
        name="product",
    )(left, right)

def on_device(valence, conduction, valence_slot_index, weights, sphere_index):
    rows = lax.axis_size("row")
    tabs = tables(2, 4)
    bands = fetch_bands(valence[0], valence_slot_index)
    plain, scaled = pick_call(arrange_p(bands), expand_q(conduction, 2), weights.reshape(-1), sphere_index, tabs)
    scaled = lax.all_to_all(scaled.reshape(rows, 2, 16, GP), "row", 0, 0, tiled=True)
    left = lax.all_gather(scaled, "col", axis=0)
    plain = lax.all_to_all(plain, "col", 0, 0, tiled=True)
    right = lax.all_gather(plain, "row", axis=0)
    return product(left, right)

def solution(mesh):
    placed = (P(BOTH, None, None), P(BOTH, None, None), P(), P(None, BOTH), P())
    return jax.shard_map(on_device, mesh=mesh, in_specs=placed, out_specs=P(None, "row", "col"), check_vma=False)
```

```python
import functools
import math
import numpy as np
import jax
import jax.numpy as jnp
from jax import lax
from jax.experimental import pallas as pl
from jax.experimental.pallas import tpu as pltpu
from jax.sharding import PartitionSpec as P

N = 40
LW = 384
LT = LW // 128
NB = 16
GB = 624
GP = 640

def split(x):
    hi = x.astype(jnp.bfloat16)
    lo = (x - hi.astype(jnp.float32)).astype(jnp.bfloat16)
    return hi, lo

def np_split(x):
    x = np.asarray(x, np.float32)
    hi = x.astype(jnp.bfloat16)
    lo = (x - hi.astype(np.float32)).astype(jnp.bfloat16)
    return hi, lo

def tables(nv, nc):
    k = np.arange(N)
    ang = 2 * np.pi * ((k[:, None] * k[None, :]) % N) / N
    c, s = np.cos(ang) / math.sqrt(N), np.sin(ang) / math.sqrt(N)
    f = np.block([[c, s], [-s, c]])
    hi, lo = np_split(f)
    axis = np.concatenate([hi, hi, lo], axis=1)
    pairs = nv * nc
    m = np.zeros((2, LW, N * 2 * pairs))
    for p in range(pairs):
        for comp in range(2):
            cols = np.arange(N) * 2 * pairs + comp * pairs + p
            for part in range(2):
                blk = f[comp * N:(comp + 1) * N, part * N:(part + 1) * N]
                m[part, p * N:(p + 1) * N][:, cols] = blk.T
    m = m.reshape(2 * LW, -1)
    mhi, mlo = np_split(m)
    last = np.stack([mhi, mlo])
    ident = np.eye(N)
    rp = np.zeros((nv * N, LW)); rq = np.zeros((nc * N, LW))
    for v in range(nv):
        for b in range(nc):
            p = v * nc + b
            rp[v * N:(v + 1) * N, p * N:(p + 1) * N] = ident
            rq[b * N:(b + 1) * N, p * N:(p + 1) * N] = ident
    return axis, last, rp.astype(jnp.bfloat16), rq.astype(jnp.bfloat16)

def stack3(x):
    hi, lo = split(x)
    return jnp.concatenate([hi, lo, hi], axis=0)

def pick_kernel(addr, order, p_ref, q_ref, sel_ref, w_ref, axis_ref, last_ref, rp_ref, *refs):
    plain_refs, scaled_refs = refs[:NB], refs[NB:NB + 8]
    d_ref, z_ref, s_ref, t_ref, hold_ref = refs[NB + 8:]
    f32 = jnp.float32
    sq = N * N
    tdims = (((0,), (0,)), ((), ()))
    pre = lax.dot_general(p_ref[0], rp_ref[...], tdims, preferred_element_type=f32)[:sq]
    pim = lax.dot_general(p_ref[1], rp_ref[...], tdims, preferred_element_type=f32)[:sq]
    qre, qim = q_ref[0].astype(f32), q_ref[1].astype(f32)
    d_ref[0] = pre * qre + pim * qim
    d_ref[1] = pre * qim - pim * qre

    def over_e(b, _):
        rows = pl.ds(pl.multiple_of(b * N, 8), N)
        x = jnp.concatenate([d_ref[0, rows, :], d_ref[1, rows, :]], axis=0)
        y = jnp.dot(axis_ref[...], stack3(x), preferred_element_type=f32)
        for c in range(2):
            for l in range(LT):
                z_ref[c, l, rows, :] = y[c * N:(c + 1) * N, l * 128:(l + 1) * 128]
        return 0
    lax.fori_loop(0, N, over_e, 0, unroll=4)

    def over_b(k, _):
        rows = pl.ds(pl.multiple_of(k * N, 8), N)
        parts = []
        for c in range(2):
            parts.append(jnp.concatenate([z_ref[c, l, pl.ds(k, N, stride=N), :] for l in range(LT)], axis=1))
        x = jnp.concatenate(parts, axis=0)
        y = jnp.dot(axis_ref[...], stack3(x), preferred_element_type=f32)
        d_ref[0, rows, :] = y[:N]
        d_ref[1, rows, :] = y[N:]
        return 0
    lax.fori_loop(0, N, over_b, 0, unroll=4)

    chunk = 320
    def over_a(i, _):
        start = pl.multiple_of(i * chunk, 8)
        x = jnp.concatenate([d_ref[0, pl.ds(start, chunk), :], d_ref[1, pl.ds(start, chunk), :]], axis=1)
        hi, lo = split(x)
        y = jnp.dot(hi, last_ref[0], preferred_element_type=f32)
        y += jnp.dot(lo, last_ref[0], preferred_element_type=f32)
        y += jnp.dot(hi, last_ref[1], preferred_element_type=f32)
        for n in range(5):
            s_ref[pl.ds(pl.multiple_of(start + n * sq, 8), chunk), :] = y[:, n * 128:(n + 1) * 128]
        return 0
    lax.fori_loop(0, sq // chunk, over_a, 0)

    for k in range(NB):
        j = order[k]
        first = j * GB
        def pick(i, _, first=first):
            base = i * 16
            for u in range(16):
                t_ref[pl.ds(base + u, 1), :] = s_ref[pl.ds(addr[first + base + u], 1), :]
            return 0
        lax.fori_loop(0, GB // 16, pick, 0)
        tt = t_ref[...].T
        sel = sel_ref[j]
        acc = jnp.zeros((16, GP), f32)
        for grp in range(8):
            acc = jnp.where(sel == grp, tt[16 * grp:16 * grp + 16], acc)
        plain_refs[k][...] = acc.astype(jnp.bfloat16)
        hold_ref[j] = (acc * w_ref[...]).astype(jnp.bfloat16)
    for k in range(8):
        for half in range(2):
            scaled_refs[k][half] = hold_ref[2 * order[NB + k] + half]

def pick_call(p, q, weights, sphere_index, order, tabs):
    axis, last, rp, _ = tabs
    sq = N * N
    ka, rest = sphere_index // sq, sphere_index % sq
    kb, ke = rest // N, rest % N
    addr = (ka // 8) * sq + ke * N + kb
    sel = jnp.pad((ka % 8).reshape(NB, 1, GB), ((0, 0), (0, 0), (0, GP - GB)), constant_values=-1)
    w = jnp.concatenate([weights, weights]).reshape(16, 1)
    vm = pl.BlockSpec(memory_space=pltpu.VMEM)
    sm = pl.BlockSpec(memory_space=pltpu.SMEM)
    outs = [jax.ShapeDtypeStruct((16, GP), jnp.bfloat16)] * NB + [jax.ShapeDtypeStruct((2, 16, GP), jnp.bfloat16)] * 8
    got = pl.pallas_call(
        pick_kernel,
        out_shape=outs,
        in_specs=[sm, sm] + [vm] * 7,
        out_specs=[vm] * len(outs),
        scratch_shapes=[
            pltpu.VMEM((2, sq, LW), jnp.float32),
            pltpu.VMEM((2, LT, sq, 128), jnp.float32),
            pltpu.VMEM((5 * sq, 128), jnp.float32),
            pltpu.VMEM((GP, 128), jnp.float32),
            pltpu.VMEM((NB, 16, GP), jnp.bfloat16),
        ],
        name="pick",
    )(addr, order, p, q, sel, w, jnp.asarray(axis), jnp.asarray(last), jnp.asarray(rp))
    return got[:NB], got[NB:]

def expand_q(conduction, nv):
    nc = conduction.shape[0]
    sq = N * N
    q = conduction.reshape(nc, 2, N, sq).transpose(1, 3, 0, 2).reshape(2, sq, nc * N)
    q = jnp.concatenate([q] * nv, axis=2)
    return jnp.pad(q, ((0, 0), (0, 0), (0, LW - q.shape[2])))

def arrange_p(bands):
    nv = bands.shape[0]
    p = bands.reshape(nv, 2, N, N * N).transpose(1, 0, 2, 3).reshape(2, nv * N, N * N)
    return jnp.pad(p, ((0, 0), (0, 0), (0, 64)))

BOTH = ("row", "col")

def fetch_bands(stored, valence_slot_index):
    devices = lax.axis_size("row") * lax.axis_size("col")
    pieces = jnp.pad(stored.reshape(-1, 128), ((0, 24), (0, 0))).reshape(devices, 8, 128)
    pieces = lax.all_to_all(pieces, BOTH, 0, 0, tiled=True)
    mine = jnp.stack([lax.dynamic_index_in_dim(pieces, valence_slot_index[v], 0, keepdims=False) for v in range(2)])
    copies = jnp.broadcast_to(mine, (devices, *mine.shape))
    spread = lax.all_to_all(copies, BOTH, 0, 0, tiled=True)
    flat = spread.transpose(1, 0, 2, 3).reshape(2, -1, 128)[:, :1000]
    return flat.reshape(2, 2, N ** 3)

ROW_OFFS = [(z, c) for z in range(4) for c in range(2)]
COL_OFFS = [(x, y) for x in range(4) for y in range(4)]

def row_send(x, dz, dc):
    perm = [(z * 2 + c, (z + dz) % 4 * 2 + (c ^ dc)) for z in range(4) for c in range(2)]
    return lax.ppermute(x, "row", perm)

def col_send(x, dx, dy):
    perm = [(a * 4 + b, (a + dx) % 4 * 4 + (b + dy) % 4) for a in range(4) for b in range(4)]
    return lax.ppermute(x, "col", perm)

def ring_gather(own, send):
    half = own.shape[0] // 2
    behind = send(own, 1)
    ahead = send(own, -1)
    far_a = send(behind[:half], 1)
    far_b = send(ahead[half:], -1)
    return behind, ahead, far_a, far_b

def spread_rows(block, first, second):
    behind, ahead, far_a, far_b = ring_gather(block, first)
    line = {0: [block], 3: [behind], 1: [ahead], 2: [far_a, far_b]}
    got = {(o, 0): line[o] for o in line}
    from_behind = {o: [second(piece, 1) for piece in line[o]] for o in (0, 3, 1, 2)}
    from_ahead = {o: [second(piece, -1) for piece in line[o]] for o in (0, 3, 1, 2)}
    for o in line:
        got[o, 3], got[o, 1] = from_behind[o], from_ahead[o]
        side, step = (from_behind, 1) if o in (0, 3) else (from_ahead, -1)
        got[o, 2] = [second(piece, step) for piece in side[o]]
    return got

def product_kernel(plan_left, plan_right, *refs):
    f32 = jnp.float32
    tdims = (((0,), (0,)), ((), ()))
    count = len(plan_left) + len(plan_right)
    ins, out_ref = refs[:count], refs[count]
    left_ref, right_ref, turned_ref, o_ref, in_sem, out_sem = refs[count + 1:]
    depth = 16 * 8 * 16

    copies = []
    for n, (s, start, size) in enumerate(plan_right):
        copies.append(pltpu.make_async_copy(ins[n], right_ref.at[pl.ds(start, size), s], in_sem.at[n]))
    for n, (half, t, start, size) in enumerate(plan_left):
        i = len(plan_right) + n
        copies.append(pltpu.make_async_copy(ins[i], left_ref.at[half, t, pl.ds(start, size)], in_sem.at[i]))
    for c in copies:
        c.start()
    for c in copies[:len(plan_right)]:
        c.wait()
    wide = right_ref[...].astype(f32)
    turned_ref[...] = jnp.concatenate([-wide[:, :, 8:], wide[:, :, :8]], axis=2).astype(jnp.bfloat16)
    stores = []
    for half in range(2):
        for c, (h, *_) in zip(copies[len(plan_right):], plan_left):
            if h == half:
                c.wait()
        left = left_ref[half].reshape(depth, GP)
        for part, ref in ((0, right_ref), (1, turned_ref)):
            y = lax.dot_general(left, ref[...].reshape(depth, GP), tdims, preferred_element_type=f32)
            n = 2 * half + part
            o_ref[n] = y[:GB, :GB]
            stores.append(pltpu.make_async_copy(o_ref.at[n], out_ref.at[part, pl.ds(half * GB, GB), :], out_sem.at[n]))
            stores[-1].start()
    for c in stores:
        c.wait()

def product(lefts, rights):
    plan_right = [(*place, a.shape[0]) for place, a in rights]
    plan_left = [(*place, a.shape[0]) for place, a in lefts]
    count = len(plan_left) + len(plan_right)
    hbm = pl.BlockSpec(memory_space=pl.ANY)
    bf16 = jnp.bfloat16
    return pl.pallas_call(
        functools.partial(product_kernel, plan_left, plan_right),
        out_shape=jax.ShapeDtypeStruct((2, 2 * GB, GB), jnp.float32),
        in_specs=[hbm] * count,
        out_specs=hbm,
        scratch_shapes=[
            pltpu.VMEM((2, 16, 8, 16, GP), bf16),
            pltpu.VMEM((16, 8, 16, GP), bf16),
            pltpu.VMEM((16, 8, 16, GP), bf16),
            pltpu.VMEM((4, GB, GB), jnp.float32),
            pltpu.SemaphoreType.DMA((count,)),
            pltpu.SemaphoreType.DMA((4,)),
        ],
        name="product",
    )(*[a for _, a in rights], *[a for _, a in lefts])

def on_device(valence, conduction, valence_slot_index, weights, sphere_index):
    row, col = lax.axis_index("row"), lax.axis_index("col")
    z, core, x, y = row // 2, row % 2, col // 4, col % 4
    order = [(x - a) % 4 * 4 + (y - b) % 4 for a, b in COL_OFFS] + [(z - a) % 4 * 2 + (core ^ c) for a, c in ROW_OFFS]
    order = jnp.stack(order).astype(jnp.int32)
    bands = fetch_bands(valence[0], valence_slot_index)
    plain, scaled = pick_call(arrange_p(bands), expand_q(conduction, 2), weights.reshape(-1), sphere_index, order, tables(2, 4))

    mine = jnp.stack([plain[0]] + [col_send(plain[k], -a, -b) for k, (a, b) in enumerate(COL_OFFS) if k])
    lead = [row_send(scaled[k], -a, c) for k, (a, c) in enumerate(ROW_OFFS) if k]
    halves = [jnp.stack([m[h] for m in [scaled[0]] + lead]) for h in range(2)]

    behind, ahead, far_a, far_b = ring_gather(mine, lambda v, d: row_send(v, d, 0))
    rights = []
    for oz, pieces in ((0, [mine]), (3, [behind]), (1, [ahead]), (2, [far_a, far_b])):
        start = 0
        for piece in pieces:
            rights.append(((oz * 2, start), piece))
            rights.append(((oz * 2 + 1, start), row_send(piece, 0, 1)))
            start += piece.shape[0]

    lefts = []
    for h in range(2):
        if h == 0:
            got = spread_rows(halves[0], lambda v, d: col_send(v, d, 0), lambda v, d: col_send(v, 0, d))
        else:
            got = spread_rows(halves[1], lambda v, d: col_send(v, 0, d), lambda v, d: col_send(v, d, 0))
        for (a, b), pieces in got.items():
            t = a * 4 + b if h == 0 else b * 4 + a
            start = 0
            for piece in pieces:
                lefts.append(((h, t, start), piece))
                start += piece.shape[0]
    return product(lefts, rights)


def solution(mesh):
    placed = (P(BOTH, None, None), P(BOTH, None, None), P(), P(None, BOTH), P())
    return jax.shard_map(on_device, mesh=mesh, in_specs=placed, out_specs=P(None, "row", "col"), check_vma=False)
```

```python
import functools
import math
import numpy as np
import jax
import jax.numpy as jnp
from jax import lax
from jax.experimental import pallas as pl
from jax.experimental.pallas import tpu as pltpu
from jax.sharding import PartitionSpec as P

N = 40
LW = 384
LT = LW // 128
NB = 16
GB = 624
GP = 640

def split(x):
    hi = x.astype(jnp.bfloat16)
    lo = (x - hi.astype(jnp.float32)).astype(jnp.bfloat16)
    return hi, lo

def np_split(x):
    x = np.asarray(x, np.float32)
    hi = x.astype(jnp.bfloat16)
    lo = (x - hi.astype(np.float32)).astype(jnp.bfloat16)
    return hi, lo

def tables(nv, nc):
    k = np.arange(N)
    ang = 2 * np.pi * ((k[:, None] * k[None, :]) % N) / N
    c, s = np.cos(ang) / math.sqrt(N), np.sin(ang) / math.sqrt(N)
    f = np.block([[c, s], [-s, c]])
    hi, lo = np_split(f)
    axis = np.concatenate([hi, hi, lo], axis=1)
    pairs = nv * nc
    m = np.zeros((2, LW, N * 2 * pairs))
    for p in range(pairs):
        for comp in range(2):
            cols = np.arange(N) * 2 * pairs + comp * pairs + p
            for part in range(2):
                blk = f[comp * N:(comp + 1) * N, part * N:(part + 1) * N]
                m[part, p * N:(p + 1) * N][:, cols] = blk.T
    m = m.reshape(2 * LW, -1)
    mhi, mlo = np_split(m)
    last = np.stack([mhi, mlo])
    ident = np.eye(N)
    rp = np.zeros((nv * N, LW)); rq = np.zeros((nc * N, LW))
    for v in range(nv):
        for b in range(nc):
            p = v * nc + b
            rp[v * N:(v + 1) * N, p * N:(p + 1) * N] = ident
            rq[b * N:(b + 1) * N, p * N:(p + 1) * N] = ident
    return axis, last, rp.astype(jnp.bfloat16), rq.astype(jnp.bfloat16)

def stack3(x):
    hi, lo = split(x)
    return jnp.concatenate([hi, lo, hi], axis=0)

def pick_kernel(addr, p_ref, q_ref, sel_ref, w_ref, axis_ref, last_ref, rp_ref, plain_ref, scaled_ref, d_ref, z_ref, s_ref, t_ref):
    f32 = jnp.float32
    sq = N * N
    tdims = (((0,), (0,)), ((), ()))
    pre = lax.dot_general(p_ref[0], rp_ref[...], tdims, preferred_element_type=f32)[:sq]
    pim = lax.dot_general(p_ref[1], rp_ref[...], tdims, preferred_element_type=f32)[:sq]
    qre, qim = q_ref[0].astype(f32), q_ref[1].astype(f32)
    d_ref[0] = pre * qre + pim * qim
    d_ref[1] = pre * qim - pim * qre

    def over_e(b, _):
        rows = pl.ds(pl.multiple_of(b * N, 8), N)
        x = jnp.concatenate([d_ref[0, rows, :], d_ref[1, rows, :]], axis=0)
        y = jnp.dot(axis_ref[...], stack3(x), preferred_element_type=f32)
        for c in range(2):
            for l in range(LT):
                z_ref[c, l, rows, :] = y[c * N:(c + 1) * N, l * 128:(l + 1) * 128]
        return 0
    lax.fori_loop(0, N, over_e, 0, unroll=4)

    def over_b(k, _):
        rows = pl.ds(pl.multiple_of(k * N, 8), N)
        parts = []
        for c in range(2):
            parts.append(jnp.concatenate([z_ref[c, l, pl.ds(k, N, stride=N), :] for l in range(LT)], axis=1))
        x = jnp.concatenate(parts, axis=0)
        y = jnp.dot(axis_ref[...], stack3(x), preferred_element_type=f32)
        d_ref[0, rows, :] = y[:N]
        d_ref[1, rows, :] = y[N:]
        return 0
    lax.fori_loop(0, N, over_b, 0, unroll=4)

    chunk = 320
    def over_a(i, _):
        start = pl.multiple_of(i * chunk, 8)
        x = jnp.concatenate([d_ref[0, pl.ds(start, chunk), :], d_ref[1, pl.ds(start, chunk), :]], axis=1)
        hi, lo = split(x)
        y = jnp.dot(hi, last_ref[0], preferred_element_type=f32)
        y += jnp.dot(lo, last_ref[0], preferred_element_type=f32)
        y += jnp.dot(hi, last_ref[1], preferred_element_type=f32)
        for n in range(5):
            s_ref[pl.ds(pl.multiple_of(start + n * sq, 8), chunk), :] = y[:, n * 128:(n + 1) * 128]
        return 0
    lax.fori_loop(0, sq // chunk, over_a, 0)

    for j in range(NB):
        def pick(i, _, j=j):
            base = i * 16
            for u in range(16):
                t_ref[pl.ds(base + u, 1), :] = s_ref[pl.ds(addr[j * GB + base + u], 1), :]
            return 0
        lax.fori_loop(0, GB // 16, pick, 0)
        tt = t_ref[...].T
        sel = sel_ref[j]
        acc = jnp.zeros((16, GP), f32)
        for grp in range(8):
            acc = jnp.where(sel == grp, tt[16 * grp:16 * grp + 16], acc)
        plain_ref[j] = acc.astype(jnp.bfloat16)
        scaled_ref[j % 2, j // 2] = (acc * w_ref[...]).astype(jnp.bfloat16)

def pick_call(p, q, weights, sphere_index, tabs):
    axis, last, rp, _ = tabs
    sq = N * N
    ka, rest = sphere_index // sq, sphere_index % sq
    kb, ke = rest // N, rest % N
    addr = (ka // 8) * sq + ke * N + kb
    sel = jnp.pad((ka % 8).reshape(NB, 1, GB), ((0, 0), (0, 0), (0, GP - GB)), constant_values=-1)
    w = jnp.concatenate([weights, weights]).reshape(16, 1)
    vm = pl.BlockSpec(memory_space=pltpu.VMEM)
    out = [jax.ShapeDtypeStruct(lead + (16, GP), jnp.bfloat16) for lead in ((NB,), (2, NB // 2))]
    return pl.pallas_call(
        pick_kernel,
        out_shape=out,
        in_specs=[pl.BlockSpec(memory_space=pltpu.SMEM)] + [vm] * 7,
        out_specs=[vm, vm],
        scratch_shapes=[
            pltpu.VMEM((2, sq, LW), jnp.float32),
            pltpu.VMEM((2, LT, sq, 128), jnp.float32),
            pltpu.VMEM((5 * sq, 128), jnp.float32),
            pltpu.VMEM((GP, 128), jnp.float32),
        ],
        name="pick",
    )(addr, p, q, sel, w, jnp.asarray(axis), jnp.asarray(last), jnp.asarray(rp))

def expand_q(conduction, nv):
    nc = conduction.shape[0]
    sq = N * N
    q = conduction.reshape(nc, 2, N, sq).transpose(1, 3, 0, 2).reshape(2, sq, nc * N)
    q = jnp.concatenate([q] * nv, axis=2)
    return jnp.pad(q, ((0, 0), (0, 0), (0, LW - q.shape[2])))

def arrange_p(bands):
    nv = bands.shape[0]
    p = bands.reshape(nv, 2, N, N * N).transpose(1, 0, 2, 3).reshape(2, nv * N, N * N)
    return jnp.pad(p, ((0, 0), (0, 0), (0, 64)))

BOTH = ("row", "col")

def fetch_bands(stored, valence_slot_index):
    devices = lax.axis_size("row") * lax.axis_size("col")
    pieces = jnp.pad(stored.reshape(-1, 128), ((0, 24), (0, 0))).reshape(devices, 8, 128)
    pieces = lax.all_to_all(pieces, BOTH, 0, 0, tiled=True)
    mine = jnp.stack([lax.dynamic_index_in_dim(pieces, valence_slot_index[v], 0, keepdims=False) for v in range(2)])
    copies = jnp.broadcast_to(mine, (devices, *mine.shape))
    spread = lax.all_to_all(copies, BOTH, 0, 0, tiled=True)
    flat = spread.transpose(1, 0, 2, 3).reshape(2, -1, 128)[:, :1000]
    return flat.reshape(2, 2, N ** 3)

RING = (0, 3, 1, 2)

def row_send(x, dz, dc):
    perm = [(z * 2 + c, (z + dz) % 4 * 2 + (c ^ dc)) for z in range(4) for c in range(2)]
    return lax.ppermute(x, "row", perm)

def col_send(x, dx, dy):
    perm = [(a * 4 + b, (a + dx) % 4 * 4 + (b + dy) % 4) for a in range(4) for b in range(4)]
    return lax.ppermute(x, "col", perm)

def ring_gather(own, send):
    half = own.shape[0] // 2
    behind = send(own, 1)
    ahead = send(own, -1)
    far_a = send(behind[:half], 1)
    far_b = send(ahead[half:], -1)
    return own, behind, ahead, far_a, far_b

def product_kernel(plan_left, plan_right, col_ref, row_ref, *refs):
    f32 = jnp.float32
    tdims = (((0,), (0,)), ((), ()))
    count = 1 + max(i for i, *_ in plan_left)
    ins, out_ref = refs[:count], refs[count]
    left_ref, right_ref, turned_ref, o_ref, in_sem, out_sem = refs[count + 1:]
    depth = 16 * 8 * 16

    copies = []
    for n, (i, start, size, first, s) in enumerate(plan_right):
        dst = right_ref.at[pl.ds(first, size), row_ref[s]]
        copies.append(pltpu.make_async_copy(ins[i].at[pl.ds(start, size)], dst, in_sem.at[n]))
    for n, (i, start, size, half, t) in enumerate(plan_left):
        dst = left_ref.at[half, col_ref[t]]
        copies.append(pltpu.make_async_copy(ins[i].at[pl.ds(start, size)], dst, in_sem.at[len(plan_right) + n]))
    for c in copies:
        c.start()
    for c in copies[:len(plan_right)]:
        c.wait()
    wide = right_ref[...].astype(f32)
    turned_ref[...] = jnp.concatenate([-wide[:, :, 8:], wide[:, :, :8]], axis=2).astype(jnp.bfloat16)
    stores = []
    for half in range(2):
        for c, entry in zip(copies[len(plan_right):], plan_left):
            if entry[3] == half:
                c.wait()
        left = left_ref[half].reshape(depth, GP)
        for part, ref in ((0, right_ref), (1, turned_ref)):
            y = lax.dot_general(left, ref[...].reshape(depth, GP), tdims, preferred_element_type=f32)
            n = 2 * half + part
            o_ref[n] = y[:GB, :GB]
            stores.append(pltpu.make_async_copy(o_ref.at[n], out_ref.at[part, pl.ds(half * GB, GB), :], out_sem.at[n]))
            stores[-1].start()
    for c in stores:
        c.wait()

def product(rights, lefts, col_order, row_order):
    arrays, plan_right, plan_left = [], [], []
    for core, pieces in enumerate(rights):
        for n, piece in enumerate(pieces):
            size = min(piece.shape[0], 16)
            for k in range(piece.shape[0] // size):
                offset = RING[k] if len(pieces) == 1 else RING[min(n, 3)]
                plan_right.append((len(arrays), k * size, size, 8 if n == 4 else 0, offset * 2 + core))
            arrays.append(piece)
    for half, pieces in enumerate(lefts):
        for n, piece in enumerate(pieces):
            for k in range(piece.shape[0] // 8):
                slow = RING[min(n, 3)]
                fast = RING[k + (2 if n == 4 else 0)]
                t = fast * 4 + slow if half == 0 else slow * 4 + fast
                plan_left.append((len(arrays), k * 8, 8, half, t))
            arrays.append(piece)
    hbm = pl.BlockSpec(memory_space=pl.ANY)
    sm = pl.BlockSpec(memory_space=pltpu.SMEM)
    bf16 = jnp.bfloat16
    return pl.pallas_call(
        functools.partial(product_kernel, plan_left, plan_right),
        out_shape=jax.ShapeDtypeStruct((2, 2 * GB, GB), jnp.float32),
        in_specs=[sm, sm] + [hbm] * len(arrays),
        out_specs=hbm,
        scratch_shapes=[
            pltpu.VMEM((2, 16, 8, 16, GP), bf16),
            pltpu.VMEM((16, 8, 16, GP), bf16),
            pltpu.VMEM((16, 8, 16, GP), bf16),
            pltpu.VMEM((4, GB, GB), jnp.float32),
            pltpu.SemaphoreType.DMA((len(plan_left) + len(plan_right),)),
            pltpu.SemaphoreType.DMA((4,)),
        ],
        name="product",
    )(col_order, row_order, *arrays)

def on_device(valence, conduction, valence_slot_index, weights, sphere_index):
    row, col = lax.axis_index("row"), lax.axis_index("col")
    z, core, x, y = row // 2, row % 2, col // 4, col % 4
    t = jnp.arange(16, dtype=jnp.int32)
    col_order = (x + t // 4) % 4 * 4 + (y + t % 4) % 4
    row_order = (z + t // 2) % 4 * 2 + (core + t) % 2
    bands = fetch_bands(valence[0], valence_slot_index)
    plain, scaled = pick_call(arrange_p(bands), expand_q(conduction, 2), weights.reshape(-1), sphere_index, tables(2, 4))

    scaled = lax.all_to_all(scaled, "row", 1, 1, tiled=True)
    plain, _ = lax.optimization_barrier((plain, scaled))
    plain = lax.all_to_all(plain, "col", 0, 0, tiled=True)

    along_x = lambda v, d: col_send(v, d, 0)
    along_y = lambda v, d: col_send(v, 0, d)
    first = jnp.concatenate(ring_gather(scaled[0], along_x))
    second = jnp.concatenate(ring_gather(scaled[1], along_y))
    lefts = [ring_gather(first, along_y), ring_gather(second, along_x)]
    column = jnp.concatenate(ring_gather(plain, lambda v, d: row_send(v, d, 0)))
    rights = [[column], [row_send(column, 0, 1)]]
    return product(rights, lefts, col_order, row_order)


def solution(mesh):
    placed = (P(BOTH, None, None), P(BOTH, None, None), P(), P(None, BOTH), P())
    return jax.shard_map(on_device, mesh=mesh, in_specs=placed, out_specs=P(None, "row", "col"), check_vma=False)
```

```python
import functools
import math
import numpy as np
import jax
import jax.numpy as jnp
from jax import lax
from jax.experimental import pallas as pl
from jax.experimental.pallas import tpu as pltpu
from jax.sharding import PartitionSpec as P


N = 40
LW = 384
LQ = 320
LT = LW // 128
NB = 16
GB = 624
GP = 640
TILES = NB * GP // 128

def split(x):
    hi = x.astype(jnp.bfloat16)
    lo = (x - hi.astype(jnp.float32)).astype(jnp.bfloat16)
    return hi, lo

def np_split(x):
    x = np.asarray(x, np.float32)
    hi = x.astype(jnp.bfloat16)
    lo = (x - hi.astype(np.float32)).astype(jnp.bfloat16)
    return hi, lo

def tables(nv, nc):
    k = np.arange(N)
    ang = 2 * np.pi * ((k[:, None] * k[None, :]) % N) / N
    c, s = np.cos(ang) / math.sqrt(N), np.sin(ang) / math.sqrt(N)
    f = np.block([[c, s], [-s, c]])
    hi, lo = np_split(f)
    axis = np.concatenate([hi, hi, lo], axis=1)
    pairs = nv * nc
    m = np.zeros((2, N, N, 2, pairs))
    for comp in range(2):
        for part in range(2):
            m[part, :, :, comp] = f[comp * N:(comp + 1) * N, part * N:(part + 1) * N].T[:, :, None]
    last = np.stack(np_split(m.reshape(2, N, 2 * pairs * N)))
    lane = np.arange(LW)
    row_a = ((lane[:, None] % N == np.arange(N)) & (lane[:, None] < pairs * N)).astype(jnp.bfloat16)
    row_pair = (lane[:, None] // N == np.arange(pairs)).astype(jnp.bfloat16)
    col_pair = (np.arange(2 * pairs * N) % pairs == np.arange(pairs)[:, None]).astype(jnp.bfloat16)
    ident = np.eye(N)
    rp = np.zeros((nv, N, LQ))
    for v in range(nv):
        for b in range(nc):
            p = v * nc + b
            rp[v, :, p * N:(p + 1) * N] = ident
    return axis, last, row_a, row_pair, col_pair, rp.astype(jnp.bfloat16)

def stack3(x):
    hi, lo = split(x)
    return jnp.concatenate([hi, lo, hi], axis=0)

def pick_kernel(addr, p_ref, q_ref, sel_ref, w_ref, axis_ref, small_ref, row_a_ref, row_pair_ref, col_pair_ref, rp_ref, plain_ref, scaled_ref,
                d_ref, z_ref, s_ref, even_ref, odd_ref, last_ref):
    f32 = jnp.float32
    sq = N * N
    tdims = (((0,), (0,)), ((), ()))

    same = jnp.dot(row_pair_ref[...], col_pair_ref[...], preferred_element_type=f32)
    for k in range(2):
        for part in range(2):
            rows = jnp.dot(row_a_ref[...], small_ref[k, part], preferred_element_type=f32)
            last_ref[k, part * LW:(part + 1) * LW, :] = (rows * same).astype(jnp.bfloat16)

    def spread(c):
        return sum(lax.dot_general(p_ref[v, c], rp_ref[v], tdims, preferred_element_type=f32) for v in range(2))

    pre, pim = spread(0), spread(1)
    qre, qim = q_ref[0].astype(f32), q_ref[1].astype(f32)
    d_ref[0, :, :LQ] = pre * qre + pim * qim
    d_ref[1, :, :LQ] = pre * qim - pim * qre
    d_ref[:, :, LQ:] = jnp.zeros((2, sq, LW - LQ), f32)

    def along_axis(planes):
        x = jnp.concatenate(planes, axis=1)
        y = jnp.dot(axis_ref[...], stack3(x), preferred_element_type=f32)
        return y[:, :LW], y[:, LW:]

    def rows_of(k):
        return pl.ds(pl.multiple_of(k * N, 8), N)

    def over_e(i, _):
        planes = [jnp.concatenate([d_ref[c, rows_of(2 * i + u), :] for c in range(2)], axis=0) for u in range(2)]
        for u, y in enumerate(along_axis(planes)):
            for c in range(2):
                for l in range(LT):
                    z_ref[c, l, rows_of(2 * i + u), :] = y[c * N:(c + 1) * N, l * 128:(l + 1) * 128]
        return 0

    lax.fori_loop(0, N // 2, over_e, 0, unroll=2)

    def over_b(i, _):
        planes = []
        for u in range(2):
            parts = [jnp.concatenate([z_ref[c, l, pl.ds(2 * i + u, N, stride=N), :] for l in range(LT)], axis=1) for c in range(2)]
            planes.append(jnp.concatenate(parts, axis=0))
        for u, y in enumerate(along_axis(planes)):
            for c in range(2):
                d_ref[c, rows_of(2 * i + u), :] = y[c * N:(c + 1) * N]
        return 0

    lax.fori_loop(0, N // 2, over_b, 0, unroll=2)

    chunk = 320

    def over_a(i, _):
        start = pl.multiple_of(i * chunk, 8)
        x = jnp.concatenate([d_ref[0, pl.ds(start, chunk), :], d_ref[1, pl.ds(start, chunk), :]], axis=1)
        hi, lo = split(x)
        y = jnp.dot(hi, last_ref[0], preferred_element_type=f32)
        y += jnp.dot(lo, last_ref[0], preferred_element_type=f32)
        y += jnp.dot(hi, last_ref[1], preferred_element_type=f32)
        for n in range(5):
            s_ref[pl.ds(pl.multiple_of(start + n * sq, 8), chunk), :] = y[:, n * 128:(n + 1) * 128]
        return 0

    lax.fori_loop(0, sq // chunk, over_a, 0)

    def pick(tile, t_ref):
        base = tile * 128
        for u in range(128):
            t_ref[pl.ds(u, 1), :] = s_ref[pl.ds(addr[base + u], 1), :]

    def finish(tile, t_ref):
        tt = t_ref[...].T
        sel = sel_ref[tile]
        acc = jnp.zeros((16, 128), f32)
        for grp in range(8):
            acc = jnp.where(sel == grp, tt[16 * grp:16 * grp + 16], acc)
        j = tile // 5
        lanes = pl.ds(pl.multiple_of((tile - 5 * j) * 128, 128), 128)
        plain_ref[j, :, lanes] = acc.astype(jnp.bfloat16)
        scaled_ref[j % 2, j // 2, :, lanes] = (acc * w_ref[...]).astype(jnp.bfloat16)

    odd_ref[...] = jnp.zeros_like(odd_ref)

    def two_tiles(i, _):
        finish(jnp.maximum(2 * i - 1, 0), odd_ref)
        pick(2 * i, even_ref)
        finish(2 * i, even_ref)
        pick(2 * i + 1, odd_ref)
        return 0

    lax.fori_loop(0, TILES // 2, two_tiles, 0)
    finish(TILES - 1, odd_ref)

def pick_call(p, q, weights, sphere_index, tabs):
    sq = N * N
    ka, rest = sphere_index // sq, sphere_index % sq
    kb, ke = rest // N, rest % N
    grow = ((0, 0), (0, GP - GB))
    addr = jnp.pad(((ka // 8) * sq + ke * N + kb).reshape(NB, GB), grow).reshape(-1)
    sel = jnp.pad((ka % 8).reshape(NB, GB), grow, constant_values=-1).reshape(TILES, 1, 128)
    w = jnp.concatenate([weights, weights]).reshape(16, 1)
    vm = pl.BlockSpec(memory_space=pltpu.VMEM)
    return pl.pallas_call(
        pick_kernel,
        out_shape=[jax.ShapeDtypeStruct(lead + (16, GP), jnp.bfloat16) for lead in ((NB,), (2, NB // 2))],
        in_specs=[pl.BlockSpec(memory_space=pltpu.SMEM)] + [vm] * (4 + len(tabs)),
        out_specs=[vm, vm],
        scratch_shapes=[
            pltpu.VMEM((2, sq, LW), jnp.float32),
            pltpu.VMEM((2, LT, sq, 128), jnp.float32),
            pltpu.VMEM((5 * sq, 128), jnp.float32),
            pltpu.VMEM((128, 128), jnp.float32),
            pltpu.VMEM((128, 128), jnp.float32),
            pltpu.VMEM((2, 2 * LW, 5 * 128), jnp.bfloat16),
        ],
        name="pick",
    )(addr, p, q, sel, w, *[jnp.asarray(t) for t in tabs])

def arrange_q(conduction, nv):
    nc = conduction.shape[0]
    sq = N * N
    q = conduction.reshape(nc, 2, N, sq).transpose(1, 3, 0, 2).reshape(2, sq, nc * N)
    return jnp.concatenate([q] * nv, axis=2)

BOTH = ("row", "col")

def fetch_bands(stored, valence_slot_index):
    devices = lax.axis_size("row") * lax.axis_size("col")
    pieces = jnp.pad(stored.reshape(-1, 128), ((0, 24), (0, 0))).reshape(devices, 8, 128)
    pieces = lax.all_to_all(pieces, BOTH, 0, 0, tiled=True)
    mine = jnp.stack([lax.dynamic_index_in_dim(pieces, valence_slot_index[v], 0, keepdims=False) for v in range(2)])
    copies = jnp.broadcast_to(mine, (devices, *mine.shape))
    spread = lax.all_to_all(copies, BOTH, 0, 0, tiled=True)
    flat = spread.transpose(1, 0, 2, 3).reshape(2, -1, 128)[:, :1000]
    return flat.reshape(2, 2, N, N * N)

RING = (0, 3, 1, 2)

def row_send(x, dz, dc):
    perm = [(z * 2 + c, (z + dz) % 4 * 2 + (c ^ dc)) for z in range(4) for c in range(2)]
    return lax.ppermute(x, "row", perm)

def col_send(x, dx, dy):
    perm = [(a * 4 + b, (a + dx) % 4 * 4 + (b + dy) % 4) for a in range(4) for b in range(4)]
    return lax.ppermute(x, "col", perm)

def ring_gather(own, send):
    half = own.shape[0] // 2

    def named(piece, step, *window):
        return send(piece[slice(*window)] if window else piece, step)

    behind = named(own, 1)
    ahead = named(own, -1)
    far_a = named(behind, 1, 0, half)
    far_b = named(ahead, -1, half, None)
    return own, behind, ahead, far_a, far_b

def ring_direct(own, send):
    got = [own]
    for step in (1, -1, 2):
        got.append(send(own, step))
    return got

def ring_halves(first, second, send):
    behind = send(first, 1)
    ahead_late = send(second, -1)
    behind_late = send(second, 1)
    ahead = send(first, -1)
    far = send(behind, 1)
    far_late = send(ahead_late, -1)
    pairs = [(0, first, second), (3, behind, behind_late), (1, ahead, ahead_late), (2, far, far_late)]
    return [(o, place, half) for o, *halves in pairs for place, half in enumerate(halves)]

def product_kernel(plan_left, plan_right, col_ref, row_ref, *refs):
    f32 = jnp.float32
    tdims = (((0,), (0,)), ((), ()))
    count = 1 + max(i for i, *_ in plan_left)
    ins, out_ref = refs[:count], refs[count]
    left_ref, right_ref, o_ref, in_sem, out_sem = refs[count + 1:]
    depth = 16 * 8 * 16

    copies = []
    for n, (i, start, size, first, s) in enumerate(plan_right):
        dst = right_ref.at[pl.ds(first, size), row_ref[s], :, pl.ds(0, GP)]
        copies.append(pltpu.make_async_copy(ins[i].at[pl.ds(start, size)], dst, in_sem.at[n]))
    for n, (i, start, size, half, t) in enumerate(plan_left):
        dst = left_ref.at[half, col_ref[t]]
        copies.append(pltpu.make_async_copy(ins[i].at[pl.ds(start, size)], dst, in_sem.at[len(plan_right) + n]))
    rights, lefts = copies[:len(plan_right)], copies[len(plan_right):]
    halves = [[c for c, entry in zip(lefts, plan_left) if entry[3] == half] for half in range(2)]
    for c in rights + halves[0]:
        c.start()
    for c in rights:
        c.wait()
    wide = right_ref[:, :, :, :GP].astype(f32)
    right_ref[:, :, :, GP:] = jnp.concatenate([-wide[:, :, 8:], wide[:, :, :8]], axis=2).astype(jnp.bfloat16)
    stores = []
    for half in range(2):
        for c in halves[half]:
            c.wait()
        if half == 0:
            for c in halves[1]:
                c.start()
        left = left_ref[half].reshape(depth, GP)
        y = lax.dot_general(left, right_ref[...].reshape(depth, 2 * GP), tdims, preferred_element_type=f32)
        for part in range(2):
            n = 2 * half + part
            o_ref[n] = y[:GB, part * GP:part * GP + GB]
            stores.append(pltpu.make_async_copy(o_ref.at[n], out_ref.at[part, pl.ds(half * GB, GB), :], out_sem.at[n]))
            stores[-1].start()
    for c in stores:
        c.wait()

def product(rights, lefts, col_order, row_order):
    arrays, plan_right, plan_left = [], [], []
    for array, owners in rights:
        for k, (offset, core) in enumerate(owners):
            plan_right.append((len(arrays), k * 16, 16, 0, offset * 2 + core))
        arrays.append(array)
    for half, pieces in enumerate(lefts):
        for slow, place, piece in pieces:
            for k in range(2):
                fast = RING[2 * place + k]
                t = fast * 4 + slow if half == 0 else slow * 4 + fast
                plan_left.append((len(arrays), k * 8, 8, half, t))
            arrays.append(piece)
    hbm = pl.BlockSpec(memory_space=pl.ANY)
    sm = pl.BlockSpec(memory_space=pltpu.SMEM)
    bf16 = jnp.bfloat16
    return pl.pallas_call(
        functools.partial(product_kernel, plan_left, plan_right),
        out_shape=jax.ShapeDtypeStruct((2, 2 * GB, GB), jnp.float32),
        in_specs=[sm, sm] + [hbm] * len(arrays),
        out_specs=hbm,
        scratch_shapes=[
            pltpu.VMEM((2, 16, 8, 16, GP), bf16),
            pltpu.VMEM((16, 8, 16, 2 * GP), bf16),
            pltpu.VMEM((4, GB, GB), jnp.float32),
            pltpu.SemaphoreType.DMA((len(plan_left) + len(plan_right),)),
            pltpu.SemaphoreType.DMA((4,)),
        ],
        name="product",
    )(col_order, row_order, *arrays)

def polarizability(valence, conduction, valence_slot_index, weights, sphere_index):
    row, col = lax.axis_index("row"), lax.axis_index("col")
    z, core, x, y = row // 2, row % 2, col // 4, col % 4
    t = jnp.arange(16, dtype=jnp.int32)
    col_order = (x + t // 4) % 4 * 4 + (y + t % 4) % 4
    row_order = (z + t // 2) % 4 * 2 + (core + t) % 2
    bands = fetch_bands(valence[0], valence_slot_index)
    plain, scaled = pick_call(bands, arrange_q(conduction, 2), weights.reshape(-1), sphere_index, tables(2, 4))

    plain = lax.all_to_all(plain, "col", 0, 0, tiled=True)
    scaled = lax.all_to_all(scaled, "row", 1, 1, tiled=True)

    along_x = lambda v, d: col_send(v, d, 0)
    along_y = lambda v, d: col_send(v, 0, d)
    lefts = []
    for block, line, cross in ((scaled[0], along_x, along_y), (scaled[1], along_y, along_x)):
        pieces = ring_direct(block, line)
        joined = [jnp.concatenate(pieces[k:k + 2]) for k in (0, 2)]
        lefts.append(ring_halves(*joined, cross))
    own, up, down, far_a, far_b = ring_gather(plain, lambda v, d: row_send(v, d, 0))
    near = jnp.concatenate([own, up, down])
    far = jnp.concatenate([far_a, far_b])
    other_near = row_send(near, 0, 1)
    other_far = row_send(far, 0, 1)
    rights = [(a, [(o, core) for o in RING[:3]]) for core, a in enumerate((near, other_near))]
    rights += [(a, [(RING[3], core)]) for core, a in enumerate((far, other_far))]
    return product(rights, lefts, col_order, row_order)


def solution(mesh):
    placed = (P(BOTH, None, None), P(BOTH, None, None), P(), P(None, BOTH), P())
    return jax.shard_map(polarizability, mesh=mesh, in_specs=placed, out_specs=P(None, "row", "col"), check_vma=False)
```
